32 devices in a mesh: frame: 8 (over z, y), head: 4 (over x, core).
Axes of the slice: x: 2, y: 2, z: 4, core: 2. Of those that a mesh axis runs over, the one named last changes fastest.
Arguments:
- latents: bfloat16 [4096, 5120], P('frame', 'head'), may hold values from -6 to 6
- queries: bfloat16 [4096, 2560], P('frame', 'head'), may hold values from -22 to 22
- keys: bfloat16 [4096, 2560], P('frame', 'head'), may hold values from -6 to 6
- values: bfloat16 [4096, 2560], P('frame', 'head'), may hold values from -6 to 6
- out_weight: bfloat16 [2560, 5120], P('head'), may hold values from -0.5 to 0.5
- gate_table: float32 [4, 5120], P(None, 'head'), may hold values from 0.5 to 2
- levels: int32 [8], P('frame'), may hold values from 0 to 3
- block_mask: int32 [8, 4], P('frame'), may hold values from 0 to 1, as said below
- fresh: bfloat16 [512, 5120], P(None, 'head'), may hold values from -6 to 6
Outputs:
- velocity: bfloat16 [4096, 5120], P('frame', 'head')
- next_latents: bfloat16 [4096, 5120], P('frame', 'head')
The draws below stay inside these ranges and needn't reach their ends.
Inputs may be any that keep to these rules, and one draw needn't show every extreme that they name: block_mask[c, 0] is 1 for every span c.
All inputs are finite; a program needn't handle non-finite values.
Results may differ from the reference program's by a relative error of at most 0.012.
Values may be sent and summed in bfloat16 or wider, within the bound.
A program may use at most 128 MiB of HBM per device.

```python
import math
import jax
import jax.numpy as jnp
from jax import lax

D = 5120
HEADS = 20
HD = 128
WIN = 4
LEVELS = 4
TOK_DEV = 512
SPANS = 8
TOKENS = 4096
HH = 2560
N_HEAD = 4


def draw_pair(key):
    key_query, key_key = jax.random.split(key, 2)
    query_draw = jnp.clip(jax.random.normal(key_query, (TOKENS, HH), jnp.float32) * 2.0, -12.0, 12.0)
    key_draw = jax.random.normal(key_key, (TOKENS, HH), jnp.float32)
    query_draw = jnp.clip(query_draw, -22.0, 22.0)
    key_draw = jnp.clip(key_draw, -6.0, 6.0)
    return (query_draw, key_draw)


def draw_queries(key, part):
    pair = draw_pair(jax.random.fold_in(key, 17))
    return pair[0].astype(jnp.bfloat16)


def draw_keys(key, part):
    pair = draw_pair(jax.random.fold_in(key, 17))
    return pair[1].astype(jnp.bfloat16)


def draw_block_mask(key, part):
    picks = jax.random.randint(jax.random.fold_in(key, 29), (SPANS, WIN), 0, 10)
    marks = (picks < 7).astype(jnp.int32)
    column = jnp.arange(WIN)[None, :]
    return jnp.where(column == 0, 1, marks).astype(jnp.int32)


def with_ends(entries, rng, smallest, high):
    dims = entries.shape
    index_at = [jax.random.randint(jax.random.fold_in(rng, axis), (), 0, dims[axis]) for axis in range(len(dims))]
    entries = entries.at[tuple(index_at)].set(smallest)
    longest = dims.index(max(dims))
    index_at[longest] = (index_at[longest] + 1) % dims[longest]
    return entries.at[tuple(index_at)].set(high)


def shard_levels(rng, extent, shards, smallest, high):
    level, own = 1.0, jax.random.fold_in(rng, 6)
    for axis_at, parts in shards:
        heights = jnp.exp(jax.random.uniform(jax.random.fold_in(own, axis_at), (parts,), jnp.float32, smallest / len(shards), high / len(shards)))
        level = level * jnp.repeat(heights, extent[axis_at] // parts).reshape([-1 if axis == axis_at else 1 for axis in range(len(extent))])
    return level


def centred(own_key, extent, deviation, reach, cuts=(), kind=jnp.bfloat16):
    entries = deviation * jax.random.normal(own_key, extent, jnp.float32)
    if cuts:
        entries = entries * shard_levels(own_key, extent, cuts, -0.22, 0.18)
    return jnp.clip(entries, -reach, reach).astype(kind)


def setup_inputs(seed: int = 0) -> dict:
    seeds = jax.random.split(jax.random.key(seed), 10)
    latents = centred(seeds[0], (TOKENS, D), 1.0, 6.0, ((0, 8), (1, 4)))
    queries = draw_queries(jax.random.fold_in(seeds[9], 71), 0)
    keys = draw_keys(jax.random.fold_in(seeds[9], 71), 0)
    values = centred(seeds[3], (TOKENS, HH), 1.0, 6.0, ((0, 8), (1, 4)))
    out_weight = centred(seeds[4], (HH, D), HD ** -0.5, 0.5, ((0, 4),))
    gate_table = jnp.clip(0.5 + 1.5 * jax.random.uniform(seeds[5], (LEVELS, D), jnp.float32) ** shard_levels(seeds[5], (LEVELS, D), ((1, 4),), -0.2, 0.2), 0.5, 2.0)
    levels = with_ends(jax.random.randint(seeds[6], (SPANS,), 0, LEVELS), jax.random.fold_in(seeds[6], 1), 0, LEVELS - 1).astype(jnp.int32)
    block_mask = draw_block_mask(jax.random.fold_in(seeds[9], 71), 0)
    fresh = centred(seeds[8], (TOK_DEV, D), 1.0, 6.0, ((1, 4),))
    return dict(latents=latents, queries=queries, keys=keys, values=values, out_weight=out_weight, gate_table=gate_table, levels=levels, block_mask=block_mask, fresh=fresh)


flow_shift = 5.0

def noise_level(point):
    return flow_shift * point / (1.0 + (flow_shift - 1.0) * point)

def reference(latents, queries, keys, values, out_weight, gate_table, levels, block_mask, fresh):
    group = HH // N_HEAD
    scale = 1.0 / math.sqrt(HD)
    padding = jnp.zeros(((WIN - 1) * TOK_DEV, HH), keys.dtype)
    key_padded = jnp.concatenate([padding, keys], 0)
    value_padded = jnp.concatenate([padding, values], 0)

    def one_span(span):
        start = (span * TOK_DEV).astype(jnp.int32)
        query_rows = lax.dynamic_slice_in_dim(queries, start, TOK_DEV, 0).astype(jnp.float32).reshape(TOK_DEV, HEADS, HD)
        key_rows = lax.dynamic_slice_in_dim(key_padded, start, WIN * TOK_DEV, 0).reshape(WIN, TOK_DEV, HEADS, HD)
        key_rows = jnp.flip(key_rows, 0).astype(jnp.float32)
        value_rows = lax.dynamic_slice_in_dim(value_padded, start, WIN * TOK_DEV, 0).reshape(WIN, TOK_DEV, HEADS, HD)
        value_rows = jnp.flip(value_rows, 0).astype(jnp.float32)
        distances = jnp.arange(WIN, dtype=jnp.int32)
        allowed = (block_mask[span] == 1) & (span - distances >= 0)
        scores = jnp.einsum('qhd,bkhd->hqbk', query_rows, key_rows) * scale
        scores = jnp.where(allowed[None, None, :, None], scores, -jnp.inf)
        top = lax.optimization_barrier(jnp.max(scores, axis=(2, 3), keepdims=True))
        expd = jnp.exp(scores - top)
        weights = (expd / lax.optimization_barrier(jnp.sum(expd, axis=(2, 3), keepdims=True))).astype(jnp.bfloat16)
        attended = jnp.einsum('hqbk,bkhd->qhd', weights.astype(jnp.float32), value_rows)
        attended = attended.reshape(TOK_DEV, HH).astype(jnp.bfloat16)
        total = jnp.zeros((TOK_DEV, D), jnp.float32)
        for index in range(N_HEAD):
            part = jnp.dot(attended[:, index * group:(index + 1) * group], out_weight[index * group:(index + 1) * group], preferred_element_type=jnp.float32)
            rounded = lax.optimization_barrier(part.astype(jnp.bfloat16))
            total = total + rounded.astype(jnp.float32)
        return total
    projected = lax.map(one_span, jnp.arange(SPANS, dtype=jnp.int32))
    level_float = levels.astype(jnp.float32)
    delta = noise_level(level_float / LEVELS) - noise_level((level_float + 1.0) / LEVELS)
    gate = gate_table[levels]
    gated = gate[:, None, :] * projected
    velocity = gated.astype(jnp.bfloat16).reshape(TOKENS, D)
    updated = latents.reshape(SPANS, TOK_DEV, D).astype(jnp.float32) + delta[:, None, None] * gated
    moved = updated[1:].reshape((SPANS - 1) * TOK_DEV, D).astype(jnp.bfloat16)
    next_latents = jnp.concatenate([moved, fresh], 0)
    return (velocity, next_latents)
```

```python
import functools
import math

import jax
import jax.numpy as jnp
from jax import lax
from jax.experimental import pallas as pl
from jax.experimental.pallas import tpu as pltpu
from jax.sharding import PartitionSpec as P


HD = 128
LEVELS = 4
CHUNKS = 4
MASKED = -1e30


flow_shift = 5.0


def shifted(value, axis, by):
    devices = lax.axis_size(axis)
    pairs = [(i, i + by) for i in range(devices) if 0 <= i + by < devices]
    return lax.ppermute(value, axis, pairs)


def swapped(value, axis, bit):
    devices = lax.axis_size(axis)
    return lax.ppermute(value, axis, [(i, i ^ bit) for i in range(devices)])


def noise_level(point):
    return flow_shift * point / (1.0 + (flow_shift - 1.0) * point)


def weights_kernel(blocks, flag_ref, q_ref, *refs):
    k_refs, v_refs = refs[:blocks], refs[blocks:2 * blocks - 1]
    acc_ref, weight_ref = refs[2 * blocks - 1:]
    query = q_ref[...]
    scale = math.log2(math.e) / math.sqrt(HD)
    scores = []
    for b in range(blocks):
        raw = lax.dot_general(
            query, k_refs[b][...], (((1,), (1,)), ((), ())), preferred_element_type=jnp.float32
        )
        scores.append(jnp.where(flag_ref[b] != 0, raw * scale, MASKED))
    top = functools.reduce(jnp.maximum, [jnp.max(s, axis=1, keepdims=True) for s in scores])
    expd = [jnp.exp2(s - top) for s in scores]
    total = sum(jnp.sum(e, axis=1, keepdims=True) for e in expd)
    inverse = 1.0 / total
    acc = sum(
        jnp.dot(expd[b].astype(jnp.bfloat16), v_refs[b][...], preferred_element_type=jnp.float32)
        for b in range(blocks - 1)
    )
    acc_ref[...] = acc * inverse
    weight_ref[...] = (expd[-1] * inverse).astype(jnp.bfloat16)


def finish_kernel(weight_ref, v_ref, acc_ref, out_ref):
    last = jnp.dot(weight_ref[...], v_ref[...], preferred_element_type=jnp.float32)
    out_ref[...] = (acc_ref[...] + last).astype(jnp.bfloat16)


def attention(flags, query, key_list, value_list):
    rows, width = query.shape
    heads = width // HD
    blocks = len(key_list)
    span = key_list[0].shape[0]
    column = pl.BlockSpec((rows, HD), lambda h: (0, h))
    key_column = pl.BlockSpec((span, HD), lambda h: (0, h))
    weight_block = pl.BlockSpec((rows, span), lambda h: (h, 0))
    params = pltpu.CompilerParams(vmem_limit_bytes=40 * 1024 * 1024)
    acc, weights = pl.pallas_call(
        functools.partial(weights_kernel, blocks),
        grid=(heads,),
        in_specs=[pl.BlockSpec(memory_space=pltpu.SMEM), column] + [key_column] * (2 * blocks - 1),
        out_specs=[column, weight_block],
        out_shape=[
            jax.ShapeDtypeStruct((rows, width), jnp.float32),
            jax.ShapeDtypeStruct((heads * rows, span), jnp.bfloat16),
        ],
        cost_estimate=pl.CostEstimate(
            flops=16 * rows * width * span * blocks,
            bytes_accessed=4 * blocks * rows * width * 2,
            transcendentals=heads * rows * span * blocks,
        ),
        compiler_params=params,
    )(flags, query, *key_list, *value_list[:-1])
    return pl.pallas_call(
        finish_kernel,
        grid=(heads,),
        in_specs=[weight_block, key_column, column],
        out_specs=column,
        out_shape=jax.ShapeDtypeStruct((rows, width), jnp.bfloat16),
        cost_estimate=pl.CostEstimate(
            flops=2 * rows * width * span, bytes_accessed=8 * rows * width, transcendentals=0
        ),
        compiler_params=params,
    )(weights, value_list[-1], acc)


def shards(latents, queries, keys, values, out_weight, gate_table, levels, block_mask, fresh):
    window = block_mask.shape[1]
    position = lax.axis_index("frame")
    frames = lax.axis_size("frame")
    distances = jnp.arange(window, dtype=jnp.int32)
    allowed = ((block_mask[0] == 1) & (position - distances >= 0)).astype(jnp.int32)

    key_at = {0: keys}
    value_at = {0: values}
    if frames % 2 == 0 and window == 4:
        odd = position % 2 == 1
        key_at[2] = shifted(keys, "frame", 2)
        value_at[2] = shifted(values, "frame", 2)
        key_at[1] = swapped(jnp.where(odd, key_at[2], keys), "frame", 1)
        value_at[1] = swapped(jnp.where(odd, value_at[2], values), "frame", 1)
        key_at[3] = shifted(key_at[1], "frame", 2)
        value_at[3] = shifted(value_at[1], "frame", 2)
    else:
        for distance in range(1, window):
            key_at[distance] = shifted(key_at[distance - 1], "frame", 1)
            value_at[distance] = shifted(value_at[distance - 1], "frame", 1)

    f32 = jnp.float32
    attended = attention(
        allowed, queries, [key_at[d] for d in range(window)], [value_at[d] for d in range(window)]
    )

    level_value = levels[0]
    picker = (jnp.arange(LEVELS, dtype=jnp.int32) == level_value).astype(f32)
    gate = jnp.dot(picker, gate_table, precision=lax.Precision.HIGHEST)
    level_float = level_value.astype(f32)
    delta = noise_level(level_float / LEVELS) - noise_level((level_float + 1.0) / LEVELS)
    is_last = position == frames - 1

    rows = queries.shape[0]
    out_width = latents.shape[1]
    heads = lax.axis_size("head")
    me = lax.axis_index("head")
    step = rows // CHUNKS
    bf16 = jnp.bfloat16
    parts = [slice(chunk * step, (chunk + 1) * step) for chunk in range(CHUNKS)]

    def project(owner):
        weight = lax.dynamic_slice_in_dim(out_weight, owner * out_width, out_width, 1)
        return jnp.dot(attended, weight, preferred_element_type=f32).astype(bf16)

    if heads == 4:
        for_pair = project(me ^ 3)
        from_pair = [swapped(for_pair[here], "head", 1) for here in parts]
        for_far = project(me ^ 2)
        from_far = [
            swapped((for_far[here].astype(f32) + from_pair[chunk].astype(f32)).astype(bf16), "head", 2)
            for chunk, here in enumerate(parts)
        ]
        for_near = project(me ^ 1)
        from_near = [swapped(for_near[here], "head", 1) for here in parts]
        own = project(me)
    else:
        whole = jnp.dot(attended, out_weight, preferred_element_type=f32).astype(bf16)
        own = lax.psum_scatter(whole, "head", scatter_dimension=1, tiled=True)
    velocities = []
    moves = []
    before = None
    for chunk, here in enumerate(parts):
        projected = own[here].astype(f32)
        if heads == 4:
            far = from_far[chunk]
            if before is not None:
                far, _ = lax.optimization_barrier((far, before))
            projected = projected + from_near[chunk].astype(f32) + far.astype(f32)
        gated = gate[None, :] * projected
        velocities.append(gated.astype(bf16))
        updated = (latents[here].astype(f32) + delta * gated).astype(bf16)
        moves.append(shifted(updated, "frame", -1))
        before = updated
    next_latents = jnp.where(is_last, fresh, jnp.concatenate(moves, 0))
    return (jnp.concatenate(velocities, 0), next_latents)


def solution(mesh):
    in_specs = (
        P("frame", "head"),
        P("frame", "head"),
        P("frame", "head"),
        P("frame", "head"),
        P("head", None),
        P(None, "head"),
        P("frame"),
        P("frame", None),
        P(None, "head"),
    )
    out_specs = (P("frame", "head"), P("frame", "head"))

    return jax.shard_map(shards, mesh=mesh, in_specs=in_specs, out_specs=out_specs, check_vma=False)
```

```python
import functools
import math

import jax
import jax.numpy as jnp
from jax import lax
from jax.experimental import pallas as pl
from jax.experimental.pallas import tpu as pltpu
from jax.sharding import PartitionSpec as P


HD = 128
LEVELS = 4
CUTS = (0, 10, 19, 27, 32)
MASKED = -1e30


flow_shift = 5.0


def shifted(value, axis, by):
    devices = lax.axis_size(axis)
    pairs = [(i, i + by) for i in range(devices) if 0 <= i + by < devices]
    return lax.ppermute(value, axis, pairs)


def swapped(value, axis, bit):
    devices = lax.axis_size(axis)
    return lax.ppermute(value, axis, [(i, i ^ bit) for i in range(devices)])


def noise_level(point):
    return flow_shift * point / (1.0 + (flow_shift - 1.0) * point)


def weights_kernel(blocks, flag_ref, q_ref, *refs):
    k_refs, v_refs = refs[:blocks], refs[blocks:2 * blocks - 1]
    acc_ref, weight_ref = refs[2 * blocks - 1:]
    query = q_ref[...]
    scale = math.log2(math.e) / math.sqrt(HD)
    scores = []
    for b in range(blocks):
        raw = lax.dot_general(
            query, k_refs[b][...], (((1,), (1,)), ((), ())), preferred_element_type=jnp.float32
        )
        scores.append(jnp.where(flag_ref[b] != 0, raw * scale, MASKED))
    top = functools.reduce(jnp.maximum, [jnp.max(s, axis=1, keepdims=True) for s in scores])
    expd = [jnp.exp2(s - top) for s in scores]
    total = sum(jnp.sum(e, axis=1, keepdims=True) for e in expd)
    inverse = 1.0 / total
    acc = sum(
        jnp.dot(expd[b].astype(jnp.bfloat16), v_refs[b][...], preferred_element_type=jnp.float32)
        for b in range(blocks - 1)
    )
    acc_ref[...] = acc * inverse
    weight_ref[...] = (expd[-1] * inverse).astype(jnp.bfloat16)


def finish_kernel(weight_ref, v_ref, acc_ref, out_ref):
    last = jnp.dot(weight_ref[...], v_ref[...], preferred_element_type=jnp.float32)
    out_ref[...] = (acc_ref[...] + last).astype(jnp.bfloat16)


def attention(flags, query, key_list, value_list):
    rows, width = query.shape
    heads = width // HD
    blocks = len(key_list)
    span = key_list[0].shape[0]
    column = pl.BlockSpec((rows, HD), lambda h: (0, h))
    key_column = pl.BlockSpec((span, HD), lambda h: (0, h))
    weight_block = pl.BlockSpec((rows, span), lambda h: (h, 0))
    params = pltpu.CompilerParams(vmem_limit_bytes=40 * 1024 * 1024)
    acc, weights = pl.pallas_call(
        functools.partial(weights_kernel, blocks),
        grid=(heads,),
        in_specs=[pl.BlockSpec(memory_space=pltpu.SMEM), column] + [key_column] * (2 * blocks - 1),
        out_specs=[column, weight_block],
        out_shape=[
            jax.ShapeDtypeStruct((rows, width), jnp.float32),
            jax.ShapeDtypeStruct((heads * rows, span), jnp.bfloat16),
        ],
        cost_estimate=pl.CostEstimate(
            flops=16 * rows * width * span * blocks,
            bytes_accessed=4 * blocks * rows * width * 2,
            transcendentals=heads * rows * span * blocks,
        ),
        compiler_params=params,
    )(flags, query, *key_list, *value_list[:-1])
    return pl.pallas_call(
        finish_kernel,
        grid=(heads,),
        in_specs=[weight_block, key_column, column],
        out_specs=column,
        out_shape=jax.ShapeDtypeStruct((rows, width), jnp.bfloat16),
        cost_estimate=pl.CostEstimate(
            flops=2 * rows * width * span, bytes_accessed=8 * rows * width, transcendentals=0
        ),
        compiler_params=params,
    )(weights, value_list[-1], acc)


def shards(latents, queries, keys, values, out_weight, gate_table, levels, block_mask, fresh):
    window = block_mask.shape[1]
    position = lax.axis_index("frame")
    frames = lax.axis_size("frame")
    distances = jnp.arange(window, dtype=jnp.int32)
    allowed = ((block_mask[0] == 1) & (position - distances >= 0)).astype(jnp.int32)

    key_at = {0: keys}
    value_at = {0: values}
    if frames % 2 == 0 and window == 4:
        odd = position % 2 == 1
        key_at[2] = shifted(keys, "frame", 2)
        value_at[2] = shifted(values, "frame", 2)
        key_at[1] = swapped(jnp.where(odd, key_at[2], keys), "frame", 1)
        value_at[1] = swapped(jnp.where(odd, value_at[2], values), "frame", 1)
        key_at[3] = shifted(key_at[1], "frame", 2)
        value_at[3] = shifted(value_at[1], "frame", 2)
    else:
        for distance in range(1, window):
            key_at[distance] = shifted(key_at[distance - 1], "frame", 1)
            value_at[distance] = shifted(value_at[distance - 1], "frame", 1)

    f32 = jnp.float32
    attended = attention(
        allowed, queries, [key_at[d] for d in range(window)], [value_at[d] for d in range(window)]
    )

    level_value = levels[0]
    picker = (jnp.arange(LEVELS, dtype=jnp.int32) == level_value).astype(f32)
    gate = jnp.dot(picker, gate_table, precision=lax.Precision.HIGHEST)
    level_float = level_value.astype(f32)
    delta = noise_level(level_float / LEVELS) - noise_level((level_float + 1.0) / LEVELS)
    is_last = position == frames - 1

    rows = queries.shape[0]
    out_width = latents.shape[1]
    heads = lax.axis_size("head")
    me = lax.axis_index("head")
    bf16 = jnp.bfloat16
    parts = [slice(rows * low // 32, rows * high // 32) for low, high in zip(CUTS, CUTS[1:])]

    def project(owner):
        weight = lax.dynamic_slice_in_dim(out_weight, owner * out_width, out_width, 1)
        return jnp.dot(attended, weight, preferred_element_type=f32).astype(bf16)

    if heads == 4:
        for_pair = project(me ^ 3)
        from_pair = []
        for here in parts:
            from_pair.append(swapped(for_pair[here], "head", 1))
        for_far = project(me ^ 2)
        from_far = []
        for chunk, here in enumerate(parts):
            both = (for_far[here].astype(f32) + from_pair[chunk].astype(f32)).astype(bf16)
            from_far.append(swapped(both, "head", 2))
        for_near = project(me ^ 1)
        from_near = [swapped(for_near[here], "head", 1) for here in parts]
        own = project(me)
    else:
        whole = jnp.dot(attended, out_weight, preferred_element_type=f32).astype(bf16)
        own = lax.psum_scatter(whole, "head", scatter_dimension=1, tiled=True)
    velocities = []
    moves = []
    before = None
    for chunk, here in enumerate(parts):
        projected = own[here].astype(f32)
        if heads == 4:
            far = from_far[chunk]
            if before is not None:
                far, _ = lax.optimization_barrier((far, before))
            projected = projected + from_near[chunk].astype(f32) + far.astype(f32)
        gated = gate[None, :] * projected
        velocities.append(gated.astype(bf16))
        updated = (latents[here].astype(f32) + delta * gated).astype(bf16)
        moves.append(shifted(updated, "frame", -1))
        before = updated
    final = parts[-1]
    most = jnp.where(is_last, fresh, jnp.concatenate(moves[:-1] + [fresh[final]], 0))
    most = lax.optimization_barrier(most)
    rest = jnp.where(is_last, fresh[final], moves[-1])
    next_latents = lax.dynamic_update_slice(most, rest, (final.start, 0))
    return (jnp.concatenate(velocities, 0), next_latents)


def solution(mesh):
    in_specs = (
        P("frame", "head"),
        P("frame", "head"),
        P("frame", "head"),
        P("frame", "head"),
        P("head", None),
        P(None, "head"),
        P("frame"),
        P("frame", None),
        P(None, "head"),
    )
    out_specs = (P("frame", "head"), P("frame", "head"))

    return jax.shard_map(shards, mesh=mesh, in_specs=in_specs, out_specs=out_specs, check_vma=False)
```
